128 devices in a mesh: coil: 16 (over x, z), frame: 8 (over y, core).
Axes of the slice: x: 4, y: 4, z: 4, core: 2. Of those that a mesh axis runs over, the one named last changes fastest.
Arguments:
- kspace: bfloat16 [32, 1024, 8, 256], P('coil', 'frame'), may hold values from -6 to 6
- sampled_lines: int32 [1024, 8], P('frame'), may hold values from 0 to 63, all different within a row
- sensitivity: float32 [32, 2, 8192], P('coil'), may hold values from -55 to 55
- dictionary: bfloat16 [32768, 2048], P('coil'), may hold values from -55 to 55
- atom_params: float32 [6, 32768], P(None, 'coil'), may hold values from -4 to 4
- concentration: float32 [8192], P('frame'), may hold values from 20 to 3000
Outputs:
- estimates: float32 [6, 8192], P(None, 'frame')
The draws below stay inside these ranges and needn't reach their ends.
Inputs may be any that keep to these rules, and one draw needn't show every extreme that they name: `sampled_lines`: each frame names 8 different lines.
All inputs are finite; a program needn't handle non-finite values.
Results may differ from the reference program's by a relative error of at most 0.0025.
The reference program's roundings to bfloat16 on the way (of `fingerprints`) count: a program that leaves them out, or rounds other values in their place, can miss the bound.
Values may be sent and summed in bfloat16 or wider, within the bound.
No kernel may reach another device: no remote copies, remote signals or barrier semaphores. Data moves between devices by JAX's collectives and lax.ppermute only.
A program may use at most 128 MiB of HBM per device.

```python
import math
import jax
import jax.numpy as jnp
from jax import lax

COILS = 32
FRAMES = 1024
NPE = 64
NRO = 128
LINES = 8
ROWS = 64
ATOMS = 32768
VOXELS = 8192


def draw_sensitivity(key, part):
    shape = (COILS, 2, VOXELS)
    values = jnp.clip(jax.random.normal(key, shape, jnp.float32), -5.5, 5.5)
    levels = jax.random.uniform(jax.random.fold_in(key, 7), (VOXELS,), jnp.float32, 0.0, math.log(10.0))
    return values * jnp.exp(levels)[None, None, :]


def draw_dictionary(key, part):
    shape = (ATOMS, 2 * FRAMES)
    values = jnp.clip(jax.random.normal(key, shape, jnp.float32), -5.5, 5.5)
    levels = jax.random.uniform(jax.random.fold_in(key, 11), (ATOMS, 1), jnp.float32, 0.0, math.log(10.0))
    return (values * jnp.exp(levels)).astype(jnp.bfloat16)


def draw_concentration(key, part):
    levels = jax.random.uniform(key, (VOXELS,), jnp.float32, math.log(20.0), math.log(100.0))
    values = jnp.exp(levels)
    return values


def level_of(own_key, extent, pieces, smallest, largest):
    level, own = 1.0, jax.random.fold_in(own_key, 6)
    for dim, blocks in pieces:
        steps = jnp.exp(jax.random.uniform(jax.random.fold_in(own, dim), (blocks,), jnp.float32, smallest / len(pieces), largest / len(pieces)))
        level = level * jnp.repeat(steps, extent[dim] // blocks).reshape([-1 if axis == dim else 1 for axis in range(len(extent))])
    return level


def picks_of(own_key, rows, number_of, top, lift):
    ranking = jax.random.permutation(jax.random.fold_in(own_key, 1), number_of)
    boost = ranking
    for power in range(3):
        boost = boost * boost // number_of
    boost = boost * lift // number_of
    lots = jax.random.randint(jax.random.fold_in(own_key, 2), (rows, number_of), 0, 4096) + boost
    fixed_rows = jax.random.permutation(jax.random.fold_in(own_key, 3), rows)[jnp.arange(number_of) % rows]
    lots = jnp.where(jnp.arange(rows)[:, None] == fixed_rows[None, :], 1 << 14, lots)
    merit = lots * number_of + jnp.arange(number_of)
    return lax.top_k(merit.astype(jnp.int32), top)[1].astype(jnp.int32)


def gaussian(key, shape, width, bound, cuts=(), held_as=jnp.bfloat16):
    drawn = width * jax.random.normal(key, shape, jnp.float32)
    if cuts:
        drawn = drawn * level_of(key, shape, cuts, -0.22, 0.18)
    return jnp.clip(drawn, -bound, bound).astype(held_as)


def setup_inputs(seed: int = 0) -> dict:
    key_of = jax.random.split(jax.random.key(seed), 7)
    kspace = gaussian(key_of[0], (COILS, FRAMES, LINES, 2 * NRO), 1.0, 6.0, ((0, 16), (1, 8)))
    sampled_lines = picks_of(key_of[1], FRAMES, NPE, LINES, 0)
    sensitivity = draw_sensitivity(jax.random.fold_in(key_of[6], 71), 0)
    dictionary = draw_dictionary(jax.random.fold_in(key_of[6], 71), 0)
    atom_params = gaussian(key_of[4], (6, ATOMS), 1.0, 4.0, ((1, 16),), jnp.float32)
    concentration = draw_concentration(jax.random.fold_in(key_of[6], 71), 0)
    return dict(kspace=kspace, sampled_lines=sampled_lines, sensitivity=sensitivity, dictionary=dictionary, atom_params=atom_params, concentration=concentration)


def readout_table(length):
    position = jnp.arange(length, dtype=jnp.int32)
    angles = (position[:, None] * position[None, :] % length).astype(jnp.float32) * (2.0 * math.pi / length)
    cos_table = jnp.cos(angles)
    sine_table = jnp.sin(angles)
    upper_half = jnp.concatenate([cos_table, sine_table], axis=1)
    lower_half = jnp.concatenate([-sine_table, cos_table], axis=1)
    return jnp.concatenate([upper_half, lower_half], axis=0).astype(jnp.bfloat16)

def line_phases(line_index, row_count, length):
    row_index = jnp.arange(row_count, dtype=jnp.int32)
    angles = (line_index[:, :, None] * row_index[None, None, :] % length).astype(jnp.float32) * (2.0 * math.pi / length)
    return (jnp.cos(angles), jnp.sin(angles))

def coil_images(samples, cos_lines, sine_lines, table):
    spread = jnp.dot(samples, table, preferred_element_type=jnp.float32)
    half_width = spread.shape[-1] // 2
    real_part = spread[..., :half_width]
    imag_part = spread[..., half_width:]
    highest = lax.Precision.HIGHEST
    image_re = jnp.einsum('fly,cflx->cfyx', cos_lines, real_part, precision=highest) - jnp.einsum('fly,cflx->cfyx', sine_lines, imag_part, precision=highest)
    image_im = jnp.einsum('fly,cflx->cfyx', sine_lines, real_part, precision=highest) + jnp.einsum('fly,cflx->cfyx', cos_lines, imag_part, precision=highest)
    return (image_re, image_im)

def combine(image_re, image_im, sensitivity):
    coil_count, frame_count, row_count, column_count = image_re.shape
    flat_re = image_re.reshape(coil_count, frame_count, row_count * column_count)
    flat_im = image_im.reshape(coil_count, frame_count, row_count * column_count)
    sens_re = sensitivity[:, 0][:, None, :]
    sens_im = sensitivity[:, 1][:, None, :]
    part_re = lax.optimization_barrier(jnp.sum(sens_re * flat_re + sens_im * flat_im, axis=0))
    part_im = lax.optimization_barrier(jnp.sum(sens_re * flat_im - sens_im * flat_re, axis=0))
    return jnp.stack([part_re, part_im], axis=1)

def atom_scales(dictionary):
    widened = dictionary.astype(jnp.float32)
    return lax.rsqrt(lax.optimization_barrier(jnp.mean(widened * widened, axis=1)) + 1e-06)

def match_stats(dictionary, atom_scale, atom_params, segment, local_kappa):
    frame_count = segment.shape[0]
    voxel_count = segment.shape[-1]
    direct = segment.reshape(2 * frame_count, voxel_count)
    turned = jnp.stack([segment[:, 1], -segment[:, 0]], axis=1).reshape(2 * frame_count, voxel_count)
    stacked = jnp.concatenate([direct, turned], axis=1)
    inner = jnp.dot(dictionary, stacked, preferred_element_type=jnp.float32)
    magnitude = jnp.sqrt(inner[:, :voxel_count] * inner[:, :voxel_count] + inner[:, voxel_count:] * inner[:, voxel_count:])
    widened = direct.astype(jnp.float32)
    voxel_scale = lax.rsqrt(lax.optimization_barrier(jnp.mean(widened * widened, axis=0)) + 1e-06)
    logits = magnitude * atom_scale[:, None] * (voxel_scale * local_kappa / (2.0 * frame_count))[None, :]
    peak_score = lax.optimization_barrier(jnp.max(logits, axis=0))
    weights = jnp.exp(logits - peak_score[None, :])
    total_weight = lax.optimization_barrier(jnp.sum(weights, axis=0))
    moments = jnp.dot(atom_params, weights, precision=lax.Precision.HIGHEST, preferred_element_type=jnp.float32)
    return (peak_score, total_weight, moments)

def reference(kspace, sampled_lines, sensitivity, dictionary, atom_params, concentration):
    cos_lines, sine_lines = line_phases(sampled_lines, ROWS, NPE)
    table = readout_table(NRO)

    def accumulate(running, coil_data):
        samples, coil_sens = coil_data
        image_re, image_im = coil_images(samples[None], cos_lines, sine_lines, table)
        return (running + combine(image_re, image_im, coil_sens[None]), None)
    start_sum = jnp.zeros((FRAMES, 2, VOXELS), jnp.float32)
    combined, _ = lax.scan(accumulate, start_sum, (kspace, sensitivity))
    fingerprints = combined.astype(jnp.bfloat16)
    atom_scale = atom_scales(dictionary)
    block_size = 256 if VOXELS % 256 == 0 else 128
    block_count = VOXELS // block_size
    blocked = jnp.moveaxis(fingerprints.reshape(FRAMES, 2, block_count, block_size), 2, 0)
    kappa_blocks = concentration.reshape(block_count, block_size)

    def one_block(inputs):
        segment, local_kappa = inputs
        peak_score, total_weight, moments = match_stats(dictionary, atom_scale, atom_params, segment, local_kappa)
        return moments / total_weight[None, :]
    results = lax.map(one_block, (blocked, kappa_blocks))
    return jnp.transpose(results, (1, 0, 2)).reshape(6, VOXELS)
```

```python
import functools
import math

import jax
import jax.numpy as jnp
from jax import lax
from jax.experimental import pallas as pl
from jax.experimental.pallas import tpu as pltpu
from jax.sharding import Mesh
from jax.sharding import PartitionSpec as P

NPE = 64
NRO = 128
ROWS = 64
LINES = 8
SIDE = 4
GROUP = 4
CHUNK = 256
TILE = 256
COIL = ("cx", "cz")
BF = jnp.bfloat16
F32 = jnp.float32
NT = (((1,), (1,)), ((), ()))


def readout_table():
    position = jnp.arange(NRO, dtype=jnp.int32)
    angles = (position[:, None] * position[None, :] % NRO).astype(F32) * (2.0 * math.pi / NRO)
    return jnp.concatenate([jnp.cos(angles), -jnp.sin(angles)], axis=1).astype(BF)


def phase_weights(line_index):
    rows = jnp.arange(ROWS, dtype=jnp.int32)
    angles = (line_index[:, :, None] * rows[None, None, :] % NPE).astype(F32) * (2.0 * math.pi / NPE)
    groups = line_index.shape[0] // GROUP
    c = jnp.cos(angles).reshape(groups, GROUP * LINES, ROWS)
    s = jnp.sin(angles).reshape(groups, GROUP * LINES, ROWS)
    base = jnp.concatenate(
        [jnp.concatenate([c, s, s, -c], axis=2), jnp.concatenate([-s, c, c, s], axis=2)], axis=1
    )
    high = lax.reduce_precision(base, 8, 7)
    return jnp.concatenate([high, base - high], axis=1).astype(BF)


def split_kernel(d_ref, q_ref, o_ref, a_ref):
    half = d_ref.shape[1] // 2
    total = jnp.zeros((d_ref.shape[0], 128), F32)
    for b in range(d_ref.shape[1] // 256):
        block = d_ref[:, 256 * b : 256 * b + 256]
        sorted_block = jnp.dot(block, q_ref[...], preferred_element_type=F32)
        o_ref[:, 128 * b : 128 * b + 128] = sorted_block[:, :128].astype(BF)
        o_ref[:, half + 128 * b : half + 128 * b + 128] = sorted_block[:, 128:].astype(BF)
        total = total + sorted_block[:, :128] * sorted_block[:, :128]
        total = total + sorted_block[:, 128:] * sorted_block[:, 128:]
    mean = jnp.sum(total, axis=1, keepdims=True) * (1.0 / d_ref.shape[1])
    a_ref[...] = jnp.broadcast_to(lax.rsqrt(mean + 1e-06), a_ref.shape)


def split_dictionary(dictionary):
    atoms, entries = dictionary.shape
    row = jnp.arange(256, dtype=jnp.int32)[:, None]
    col = jnp.arange(256, dtype=jnp.int32)[None, :]
    q = (row == 2 * (col % 128) + col // 128).astype(BF)
    return pl.pallas_call(
        split_kernel,
        grid=(atoms // TILE,),
        in_specs=[
            pl.BlockSpec((TILE, entries), lambda i: (i, 0)),
            pl.BlockSpec((256, 256), lambda i: (0, 0)),
        ],
        out_specs=[
            pl.BlockSpec((TILE, entries), lambda i: (i, 0)),
            pl.BlockSpec((TILE, 128), lambda i: (i, 0)),
        ],
        out_shape=[
            jax.ShapeDtypeStruct((atoms, entries), BF),
            jax.ShapeDtypeStruct((atoms, 128), F32),
        ],
        cost_estimate=pl.CostEstimate(
            flops=2 * atoms * entries * 256, transcendentals=0, bytes_accessed=atoms * entries * 4
        ),
        name="split_dictionary",
    )(dictionary, q)


def readout_kernel(k_ref, t_ref, s_ref, o_ref):
    coils, rows, _ = k_ref.shape
    dests = o_ref.shape[0]
    per = GROUP * LINES
    step = 4
    low_lane = lax.broadcasted_iota(jnp.int32, (NRO, step * 128), 1) % 128 < 64

    def some_groups(i, carry):
        pieces = []
        for c in range(coils):
            k = k_ref[c, pl.ds(pl.multiple_of(i * step * per, step * per), step * per), :]
            turned = jnp.concatenate([k[:, NRO:], -k[:, :NRO]], axis=1)
            k = k.reshape(step, per, 2 * NRO)
            turned = turned.reshape(step, per, 2 * NRO)
            stacked = jnp.stack([k, turned, k, turned], axis=1).reshape(step * 128, 2 * NRO)
            out = lax.dot_general(t_ref[...], stacked, NT, preferred_element_type=F32)
            high = out.astype(BF).astype(F32)
            pieces.append(jnp.where(low_lane, high, out - high))
        lanes = pl.ds(pl.multiple_of(i * step * 128, step * 128), step * 128)
        for d in range(dests):
            both = jnp.concatenate([p[8 * d : 8 * d + 8] for p in pieces], axis=0)
            o_ref[d, :, lanes] = both.astype(BF)
        return carry

    lax.fori_loop(0, rows // (step * per), some_groups, 0)
    base = rows // per * 128
    for r in range(2):
        pieces = []
        for c in range(coils):
            s = s_ref[c, r]
            high = s.astype(BF).astype(F32)
            pieces.append(jnp.concatenate([high, s - high], axis=0).T)
        for d in range(dests):
            both = jnp.concatenate([p[8 * d : 8 * d + 8] for p in pieces], axis=0)
            o_ref[d, :, base + 128 * r : base + 128 * r + 128] = both.astype(BF)


def transform_readout(kspace, sensitivity):
    coils, frames = kspace.shape[:2]
    width = frames // GROUP * 128 + 256
    return pl.pallas_call(
        readout_kernel,
        out_shape=jax.ShapeDtypeStruct((SIDE * SIDE, coils * 8, width), BF),
        name="transform_readout",
    )(
        kspace.reshape(coils, frames * LINES, 2 * NRO),
        readout_table(),
        sensitivity.reshape(coils, 2, ROWS, NRO),
    )


def recon_kernel(r_ref, w_ref, o_ref, s1_ref, s2_ref, comb_ref):
    sources, sub, width = r_ref.shape
    rows = sources * sub
    coils = rows // 8
    groups = (width - 256) // 128
    for r, ref in ((0, s1_ref), (1, s2_ref)):
        at = width - 256 + 128 * r
        parts = r_ref[:, :, at : at + 128].reshape(rows, 128).astype(F32)
        ref[...] = parts + pltpu.roll(parts, 64, 1)
    frame_of_row = lax.broadcasted_iota(jnp.int32, (64, 256), 0) // LINES % GROUP
    zero = jnp.zeros((64, 256), BF)

    def one_group(g, carry):
        lhs = r_ref[:, :, pl.ds(pl.multiple_of(g * 128, 128), 128)].reshape(rows, 128)
        lhs = jnp.concatenate([lhs, lhs], axis=1)
        high = w_ref[g, :64]
        low = w_ref[g, 64:]
        for j in range(GROUP):
            mine = frame_of_row == j
            h = jnp.where(mine, high, zero)
            w = jnp.concatenate([h, h, jnp.where(mine, low, zero), zero], axis=0)
            image = jnp.dot(lhs, w, preferred_element_type=F32)
            total = s1_ref[...] * image[:, :128] + s2_ref[...] * image[:, 128:]
            comb_ref[pl.ds(pl.multiple_of((g * GROUP + j) * 8, 8), 8), :] = jnp.sum(
                total.reshape(coils, 8, 128), axis=0
            )
        return carry

    lax.fori_loop(0, groups, one_group, 0)
    frames = groups * GROUP
    for pair in range(4):
        t = [comb_ref[pl.ds(2 * pair + k, frames, stride=8), :].T for k in range(2)]
        half, at = pair // 2, pair % 2 * 16
        for dest in range(o_ref.shape[0]):
            for r in range(2):
                y = r * ROWS + 8 * dest
                both = jnp.concatenate([t[0][y : y + 8], t[1][y : y + 8]], axis=0)
                o_ref[dest, half, r, at : at + 16, :] = both.astype(BF)


def reconstruct(received, weights, peers):
    sources, sub, width = received.shape
    frames = (width - 256) // 128 * GROUP
    rows = sources * sub
    return pl.pallas_call(
        recon_kernel,
        out_shape=jax.ShapeDtypeStruct((peers, 2, 2, 32, frames), BF),
        scratch_shapes=[
            pltpu.VMEM((rows, 128), F32),
            pltpu.VMEM((rows, 128), F32),
            pltpu.VMEM((frames * 8, 128), F32),
        ],
        name="reconstruct",
    )(received, weights)


def match_kernel(place, at_ref, d_ref, a_ref, p_ref, ca_ref, cb_ref, *refs):
    pieces = refs[: len(place)]
    o_ref, r_ref, u_ref, b0_ref, b1_ref, m_ref, acc_ref = refs[len(place) :]
    step = pl.program_id(0)
    half = r_ref.shape[1] // 2
    span = half // pieces[0].shape[1]

    @pl.when(step == 0)
    def _():
        for ref, (kind, first) in zip(pieces, place):
            for i in range(ref.shape[0]):
                position = at_ref[kind * SIDE + first + i]
                row = pl.multiple_of(kind * 128 + position * 32, 32)
                for f in range(ref.shape[1]):
                    re = ref[i, f, 0]
                    im = ref[i, f, 1]
                    a, b = span * f, half + span * f
                    r_ref[pl.ds(row, 32), a : a + span] = re
                    r_ref[pl.ds(row, 32), b : b + span] = im
                    r_ref[pl.ds(CHUNK + row, 32), a : a + span] = im
                    r_ref[pl.ds(CHUNK + row, 32), b : b + span] = -re
        total = jnp.zeros((CHUNK, 128), F32)
        for k in range(2 * half // 128):
            x = r_ref[:CHUNK, 128 * k : 128 * k + 128].astype(F32)
            total = total + x * x
        mean = jnp.sum(total, axis=1, keepdims=True) * (1.0 / (2 * half))
        scale = lax.rsqrt(mean + 1e-06) * (1.0 / (2 * half))
        wide = jnp.broadcast_to(scale, (CHUNK, 128)).T
        kappa = jnp.concatenate([ca_ref[0], cb_ref[0]], axis=1)
        u_ref[...] = wide[:8] * kappa
        m_ref[...] = jnp.zeros_like(m_ref)
        acc_ref[...] = jnp.zeros_like(acc_ref)
        b1_ref[...] = jnp.zeros_like(b1_ref)

    u = u_ref[:1]

    def inner(tile, ref):
        ref[...] = lax.dot_general(
            d_ref[TILE * tile : TILE * tile + TILE], r_ref[...], NT, preferred_element_type=F32
        )

    def weigh(ref, scale, params):
        re = ref[:, :CHUNK]
        im = ref[:, CHUNK:]
        logits = jnp.sqrt(re * re + im * im) * jnp.concatenate([scale, scale], axis=1) * u
        old = m_ref[:1]
        top = jnp.maximum(old, jnp.max(logits, axis=0, keepdims=True))
        m_ref[...] = jnp.broadcast_to(top, m_ref.shape)
        weights = jnp.exp(logits - top)
        high = weights.astype(BF)
        low = (weights - high.astype(F32)).astype(BF)
        acc_ref[...] = (
            acc_ref[...] * jnp.exp(old - top)
            + jnp.dot(params, high, preferred_element_type=F32)
            + jnp.dot(params, low, preferred_element_type=F32)
        )

    inner(0, b0_ref)
    weigh(b1_ref, a_ref[step, 0], p_ref[step, 0])
    inner(1, b1_ref)
    weigh(b0_ref, a_ref[step, 1], p_ref[step, 1])

    @pl.when(step == pl.num_programs(0) - 1)
    def _():
        weigh(b1_ref, a_ref[step + 1, 0], p_ref[step + 1, 0])
        acc = acc_ref[...]
        sums = acc[:8] + acc[8:]
        row = lax.broadcasted_iota(jnp.int32, sums.shape, 0)
        o_ref[...] = jnp.where(row == 7, m_ref[...], sums)


def match(dictionary, atom_scale, params, kappa_a, kappa_b, where, pieces, place, cycle):
    atoms, entries = dictionary.shape
    steps = atoms // (2 * TILE)
    whole = lambda x: pl.BlockSpec(x.shape, lambda i, at, n=x.ndim: (0,) * n)
    return pl.pallas_call(
        functools.partial(match_kernel, place),
        grid_spec=pltpu.PrefetchScalarGridSpec(
            num_scalar_prefetch=1,
            grid=(steps,),
            in_specs=[
                pl.BlockSpec((2 * TILE, entries), lambda i, at: (i, 0)),
                whole(atom_scale),
                whole(params),
                pl.BlockSpec((1, 1, 128), lambda i, at: (at[2 * SIDE], 0, 0)),
                pl.BlockSpec((1, 1, 128), lambda i, at: (at[2 * SIDE + 1], 0, 0)),
                *[whole(x) for x in pieces],
            ],
            out_specs=pl.BlockSpec((8, CHUNK), lambda i, at: (0, 0)),
            scratch_shapes=[
                pltpu.VMEM((2 * CHUNK, entries), BF),
                pltpu.VMEM((8, CHUNK), F32),
                pltpu.VMEM((TILE, 2 * CHUNK), F32),
                pltpu.VMEM((TILE, 2 * CHUNK), F32),
                pltpu.VMEM((8, CHUNK), F32),
                pltpu.VMEM((16, CHUNK), F32),
            ],
        ),
        out_shape=jax.ShapeDtypeStruct((8, CHUNK), F32),
        compiler_params=pltpu.CompilerParams(dimension_semantics=("arbitrary",)),
        cost_estimate=pl.CostEstimate(
            flops=4 * atoms * entries * CHUNK,
            transcendentals=2 * atoms * CHUNK,
            bytes_accessed=atoms * entries * 2 + entries * CHUNK * 2,
        ),
        name="match",
    )(where, dictionary, atom_scale, params, kappa_a, kappa_b, *pieces)


ORDER = (0, -1, 1, 2)


def finish_kernel(s_ref, o_ref):
    for kind in range(2):
        for place in range(SIDE):
            parts = []
            for source in range(SIDE * SIDE):
                own = source % SIDE if kind == 0 else source // SIDE
                k = ORDER.index((place - own + 1) % SIDE - 1)
                parts.append(s_ref[source, k, :, 128 * kind : 128 * kind + 128])
            top = parts[0][7:8]
            for p in parts[1:]:
                top = jnp.maximum(top, p[7:8])
            total = jnp.zeros_like(parts[0])
            for p in parts:
                total = total + p * jnp.exp(p[7:8] - top)
            at = (kind * SIDE + place) * 128
            o_ref[:, at : at + 128] = total / total[6:7]


def finish(stats):
    return pl.pallas_call(
        finish_kernel,
        out_shape=jax.ShapeDtypeStruct((8, 2 * SIDE * 128), F32),
        name="finish",
    )(stats)


def shift(v, axis, by):
    return lax.ppermute(v, axis, [(i, (i + by) % SIDE) for i in range(SIDE)])


def body(kspace, sampled_lines, sensitivity, dictionary, atom_params, concentration):
    peers = lax.axis_size("frame")
    mx, mz = lax.axis_index("cx"), lax.axis_index("cz")
    outgoing = transform_readout(kspace, sensitivity)
    received = lax.all_to_all(outgoing, COIL, split_axis=0, concat_axis=0, tiled=True)

    split, atom_scale = split_dictionary(dictionary)
    atoms = dictionary.shape[0]
    pairs = atoms // (2 * TILE)
    atom_scale = jnp.pad(atom_scale.reshape(2 * pairs, TILE, 128), ((1, 1), (0, 0), (0, 0)))
    atom_scale = atom_scale.reshape(pairs + 1, 2, TILE, 128)
    high = lax.reduce_precision(atom_params, 8, 7)
    ones = jnp.ones((1, atoms), F32)
    none = jnp.zeros((1, atoms), F32)
    params = jnp.concatenate([high, ones, none, atom_params - high, none, none], axis=0).astype(BF)
    params = jnp.moveaxis(params.reshape(16, 2 * pairs, TILE), 1, 0)
    params = jnp.pad(params, ((1, 1), (0, 0), (0, 0))).reshape(pairs + 1, 2, 16, TILE)
    weights = phase_weights(sampled_lines)
    kappa = concentration.reshape(8, SIDE, SIDE, 2, 4)
    kappa_a = kappa[:, :, :, 0].transpose(2, 1, 3, 0).reshape(SIDE, 1, 128)
    kappa_b = kappa[:, :, :, 1].transpose(1, 2, 3, 0).reshape(SIDE, 1, 128)
    order = jnp.array(ORDER, dtype=jnp.int32)
    at_x = (mx + order) % SIDE
    at_z = (mz + order) % SIDE

    sent = reconstruct(received, weights, peers)
    shares = lax.all_to_all(sent, "frame", split_axis=0, concat_axis=0, tiled=True)

    def first(v, axis):
        return jnp.stack([v, shift(v, axis, 1), shift(v, axis, -1), shift(v, axis, 2)])

    a = first(shares[:, 0], "cx")
    b = first(shares[:, 1], "cz")
    a_less, b_less = shift(a, "cz", 1), shift(b, "cx", 1)
    a_more, b_more = shift(a, "cz", -1), shift(b, "cx", -1)
    a_far = [shift(a_less[:2], "cz", 1), shift(a_more[2:], "cz", -1)]
    b_far = [shift(b_less[:2], "cx", 1), shift(b_more[2:], "cx", -1)]

    def chunk(k, pieces, place):
        where = jnp.concatenate([at_x, at_z, at_z[k : k + 1], at_x[k : k + 1]])
        return match(split, atom_scale, params, kappa_a, kappa_b, where, pieces, place, k)

    two = ((0, 0), (1, 0))
    stats = [
        chunk(0, [a, b], two),
        chunk(1, [a_less, b_less], two),
        chunk(2, [a_more, b_more], two),
        chunk(3, [*a_far, *b_far], ((0, 0), (0, 2), (1, 0), (1, 2))),
    ]
    stats = jnp.stack(stats)
    sources = SIDE * SIDE
    stats = lax.all_to_all(
        jnp.broadcast_to(stats[None], (sources, *stats.shape)), COIL, 0, 0, tiled=True
    )
    found = finish(stats)[:6].reshape(6, 2, SIDE, SIDE, 4, 8)
    a = found[:, 0].transpose(0, 4, 2, 1, 3)
    b = found[:, 1].transpose(0, 4, 1, 2, 3)
    return jnp.stack([a, b], axis=4).reshape(6, 8 * NRO)


def solution(mesh):
    split = Mesh(mesh.devices.reshape(SIDE, SIDE, mesh.shape["frame"]), (*COIL, "frame"))
    return jax.shard_map(
        body,
        mesh=split,
        in_specs=(
            P(COIL, "frame", None, None),
            P("frame", None),
            P(COIL, None, None),
            P(COIL, None),
            P(None, COIL),
            P("frame"),
        ),
        out_specs=P(None, "frame"),
        check_vma=False,
    )
```

```python
import functools
import math

import jax
import jax.numpy as jnp
from jax import lax
from jax.experimental import pallas as pl
from jax.experimental.pallas import tpu as pltpu
from jax.sharding import Mesh
from jax.sharding import PartitionSpec as P

NPE = 64
NRO = 128
ROWS = 64
LINES = 8
SIDE = 4
GROUP = 4
CHUNK = 256
TILE = 256
STEP = 2 * TILE
COIL = ("cx", "cz")
BF = jnp.bfloat16
F32 = jnp.float32
NT = (((1,), (1,)), ((), ()))


def readout_table():
    position = jnp.arange(NRO, dtype=jnp.int32)
    angles = (position[:, None] * position[None, :] % NRO).astype(F32) * (2.0 * math.pi / NRO)
    return jnp.concatenate([jnp.cos(angles), -jnp.sin(angles)], axis=1).astype(BF)


def phase_weights(line_index):
    rows = jnp.arange(ROWS, dtype=jnp.int32)
    angles = (line_index[:, :, None] * rows[None, None, :] % NPE).astype(F32) * (2.0 * math.pi / NPE)
    groups = line_index.shape[0] // GROUP
    c = jnp.cos(angles).reshape(groups, GROUP * LINES, ROWS)
    s = jnp.sin(angles).reshape(groups, GROUP * LINES, ROWS)
    base = jnp.concatenate(
        [jnp.concatenate([c, s, s, -c], axis=2), jnp.concatenate([-s, c, c, s], axis=2)], axis=1
    )
    high = lax.reduce_precision(base, 8, 7)
    return jnp.concatenate([high, base - high], axis=1).astype(BF)


def split_kernel(d_ref, q_ref, o_ref, a_ref):
    entries = d_ref.shape[1]
    half = entries // 2
    total = jnp.zeros((8, d_ref.shape[0]), F32)
    for b in range(entries // 256):
        block = d_ref[:, 256 * b : 256 * b + 256]
        turned = lax.dot_general(q_ref[...], block, NT, preferred_element_type=F32)
        o_ref[0, 128 * b : 128 * b + 128] = turned[:128].astype(BF)
        o_ref[0, half + 128 * b : half + 128 * b + 128] = turned[128:].astype(BF)
        total = total + jnp.sum((turned * turned).reshape(32, 8, -1), axis=0)
    mean = jnp.sum(total, axis=0, keepdims=True) * (1.0 / entries)
    a_ref[0] = jnp.broadcast_to(lax.rsqrt(mean + 1e-06), a_ref.shape[1:])


def split_dictionary(dictionary):
    atoms, entries = dictionary.shape
    row = jnp.arange(256, dtype=jnp.int32)[:, None]
    col = jnp.arange(256, dtype=jnp.int32)[None, :]
    q = (col == 2 * (row % 128) + row // 128).astype(BF)
    steps = atoms // STEP
    return pl.pallas_call(
        split_kernel,
        grid=(steps,),
        in_specs=[
            pl.BlockSpec((STEP, entries), lambda i: (i, 0)),
            pl.BlockSpec((256, 256), lambda i: (0, 0)),
        ],
        out_specs=[
            pl.BlockSpec((1, entries, STEP), lambda i: (i, 0, 0)),
            pl.BlockSpec((1, 8, STEP), lambda i: (i, 0, 0)),
        ],
        out_shape=[
            jax.ShapeDtypeStruct((steps, entries, STEP), BF),
            jax.ShapeDtypeStruct((steps, 8, STEP), F32),
        ],
        cost_estimate=pl.CostEstimate(
            flops=2 * atoms * entries * 256, transcendentals=0, bytes_accessed=atoms * entries * 4
        ),
        name="split_dictionary",
    )(dictionary, q)


def readout_kernel(k_ref, t_ref, s_ref, o_ref):
    coils, rows, _ = k_ref.shape
    dests = o_ref.shape[0]
    per = GROUP * LINES
    step = 4
    low_lane = lax.broadcasted_iota(jnp.int32, (NRO, step * 128), 1) % 128 < 64

    def some_groups(i, carry):
        pieces = []
        for c in range(coils):
            k = k_ref[c, pl.ds(pl.multiple_of(i * step * per, step * per), step * per), :]
            turned = jnp.concatenate([k[:, NRO:], -k[:, :NRO]], axis=1)
            k = k.reshape(step, per, 2 * NRO)
            turned = turned.reshape(step, per, 2 * NRO)
            stacked = jnp.stack([k, turned, k, turned], axis=1).reshape(step * 128, 2 * NRO)
            out = lax.dot_general(t_ref[...], stacked, NT, preferred_element_type=F32)
            high = out.astype(BF).astype(F32)
            pieces.append(jnp.where(low_lane, high, out - high))
        lanes = pl.ds(pl.multiple_of(i * step * 128, step * 128), step * 128)
        for d in range(dests):
            both = jnp.concatenate([p[8 * d : 8 * d + 8] for p in pieces], axis=0)
            o_ref[d, :, lanes] = both.astype(BF)
        return carry

    lax.fori_loop(0, rows // (step * per), some_groups, 0)
    base = rows // per * 128
    for r in range(2):
        pieces = []
        for c in range(coils):
            s = jnp.concatenate(
                [s_ref[c, r : r + 1, NRO * y : NRO * y + NRO] for y in range(ROWS)], axis=0
            )
            high = s.astype(BF).astype(F32)
            pieces.append(jnp.concatenate([high, s - high], axis=0).T)
        for d in range(dests):
            both = jnp.concatenate([p[8 * d : 8 * d + 8] for p in pieces], axis=0)
            o_ref[d, :, base + 128 * r : base + 128 * r + 128] = both.astype(BF)


def transform_readout(kspace, sensitivity):
    coils, frames = kspace.shape[:2]
    width = frames // GROUP * 128 + 256
    return pl.pallas_call(
        readout_kernel,
        out_shape=jax.ShapeDtypeStruct((SIDE * SIDE, coils * 8, width), BF),
        name="transform_readout",
    )(
        kspace.reshape(coils, frames * LINES, 2 * NRO),
        readout_table(),
        sensitivity,
    )


def recon_kernel(r_ref, w_ref, o_ref, s1_ref, s2_ref, comb_ref):
    sources, sub, width = r_ref.shape
    rows = sources * sub
    coils = rows // 8
    groups = (width - 256) // 128
    for r, ref in ((0, s1_ref), (1, s2_ref)):
        at = width - 256 + 128 * r
        parts = r_ref[:, :, at : at + 128].reshape(rows, 128).astype(F32)
        ref[...] = parts + pltpu.roll(parts, 64, 1)
    frame_of_row = lax.broadcasted_iota(jnp.int32, (64, 256), 0) // LINES % GROUP
    zero = jnp.zeros((64, 256), BF)

    def one_group(g):
        lhs = r_ref[:, :, pl.ds(pl.multiple_of(g * 128, 128), 128)].reshape(rows, 128)
        lhs = jnp.concatenate([lhs, lhs], axis=1)
        high = w_ref[g, :64]
        low = w_ref[g, 64:]
        for j in range(GROUP):
            mine = frame_of_row == j
            h = jnp.where(mine, high, zero)
            w = jnp.concatenate([h, h, jnp.where(mine, low, zero), zero], axis=0)
            image = jnp.dot(lhs, w, preferred_element_type=F32)
            total = s1_ref[...] * image[:, :128] + s2_ref[...] * image[:, 128:]
            comb_ref[pl.ds(pl.multiple_of((g * GROUP + j) * 8, 8), 8), :] = jnp.sum(
                total.reshape(coils, 8, 128), axis=0
            )

    def two_groups(i, carry):
        one_group(2 * i)
        one_group(2 * i + 1)
        return carry

    lax.fori_loop(0, groups // 2, two_groups, 0)
    frames = groups * GROUP
    for pair in range(4):
        t = [comb_ref[pl.ds(2 * pair + k, frames, stride=8), :].T for k in range(2)]
        half, at = pair // 2, pair % 2 * 16
        for dest in range(o_ref.shape[0]):
            for r in range(2):
                y = r * ROWS + 8 * dest
                both = jnp.concatenate([t[0][y : y + 8], t[1][y : y + 8]], axis=0)
                o_ref[dest, half, r, at : at + 16, :] = both.astype(BF)


def reconstruct(received, weights, peers):
    sources, sub, width = received.shape
    frames = (width - 256) // 128 * GROUP
    rows = sources * sub
    return pl.pallas_call(
        recon_kernel,
        out_shape=jax.ShapeDtypeStruct((peers, 2, 2, 32, frames), BF),
        scratch_shapes=[
            pltpu.VMEM((rows, 128), F32),
            pltpu.VMEM((rows, 128), F32),
            pltpu.VMEM((frames * 8, 128), F32),
        ],
        name="reconstruct",
    )(received, weights)


def match_kernel(place, at, at_ref, d_ref, a_ref, p_ref, ca_ref, cb_ref, *refs):
    pieces = refs[: len(place)]
    o_ref, r_ref, u_ref, b0_ref, b1_ref, m_ref, acc_ref = refs[len(place) :]
    step = pl.program_id(0)
    half = r_ref.shape[1] // 2
    span = half // pieces[0].shape[1]

    @pl.when(step == 0)
    def _():
        for ref, (kind, first) in zip(pieces, place):
            for i in range(ref.shape[0]):
                position = at_ref[at + kind * SIDE + first + i]
                row = pl.multiple_of(kind * 128 + position * 32, 32)
                for f in range(ref.shape[1]):
                    re = ref[i, f, 0]
                    im = ref[i, f, 1]
                    a, b = span * f, half + span * f
                    r_ref[pl.ds(row, 32), a : a + span] = re
                    r_ref[pl.ds(row, 32), b : b + span] = im
                    r_ref[pl.ds(CHUNK + row, 32), a : a + span] = im
                    r_ref[pl.ds(CHUNK + row, 32), b : b + span] = -re
        total = jnp.zeros((CHUNK, 128), F32)
        for k in range(2 * half // 128):
            x = r_ref[:CHUNK, 128 * k : 128 * k + 128].astype(F32)
            total = total + x * x
        mean = jnp.sum(total, axis=1, keepdims=True) * (1.0 / (2 * half))
        scale = lax.rsqrt(mean + 1e-06) * (1.0 / (2 * half))
        kappa = jnp.concatenate([ca_ref[0], cb_ref[0]], axis=1)
        kappa = jnp.broadcast_to(kappa, (128, CHUNK)).T
        u_ref[...] = scale * kappa
        m_ref[...] = jnp.zeros_like(m_ref)
        acc_ref[...] = jnp.zeros_like(acc_ref)
        b1_ref[...] = jnp.zeros_like(b1_ref)

    def inner(part, ref):
        ref[...] = jnp.dot(
            r_ref[...], d_ref[0, :, TILE * part : TILE * part + TILE], preferred_element_type=F32
        )

    def weigh(ref, scale, params):
        u = u_ref[...]
        re = ref[:CHUNK]
        im = ref[CHUNK:]
        logits = jnp.sqrt(re * re + im * im) * scale * jnp.concatenate([u, u], axis=1)
        old = m_ref[...]
        top = jnp.max(jnp.maximum(logits[:, :128], logits[:, 128:]), axis=1, keepdims=True)
        top = jnp.maximum(old, top)
        m_ref[...] = top
        weights = jnp.exp(logits - jnp.concatenate([top, top], axis=1))
        high = weights.astype(BF)
        low = (weights - high.astype(F32)).astype(BF)
        acc_ref[...] = (
            acc_ref[...] * jnp.exp(old - top)
            + jnp.dot(high, params, preferred_element_type=F32)
            + jnp.dot(low, params, preferred_element_type=F32)
        )

    before = jnp.maximum(step - 1, 0)
    counts = (step > 0).astype(F32)
    inner(0, b0_ref)
    weigh(b1_ref, a_ref[before, :1, TILE:], (p_ref[before, 1].astype(F32) * counts).astype(BF))
    inner(1, b1_ref)
    weigh(b0_ref, a_ref[step, :1, :TILE], p_ref[step, 0])

    @pl.when(step == pl.num_programs(0) - 1)
    def _():
        weigh(b1_ref, a_ref[step, :1, TILE:], p_ref[step, 1])
        acc = acc_ref[...].T
        sums = acc[:8] + acc[8:16]
        row = lax.broadcasted_iota(jnp.int32, sums.shape, 0)
        o_ref[...] = jnp.where(row == 7, m_ref[...].T[:8], sums)


def match(dictionary, atom_scale, params, kappa_a, kappa_b, where, pieces, place, chunk):
    steps, entries, _ = dictionary.shape
    atoms = steps * STEP
    stride = 2 * SIDE + 2
    at = chunk * stride
    whole = lambda x: pl.BlockSpec(x.shape, lambda i, w, n=x.ndim: (0,) * n)
    return pl.pallas_call(
        functools.partial(match_kernel, place, at),
        grid_spec=pltpu.PrefetchScalarGridSpec(
            num_scalar_prefetch=1,
            grid=(steps,),
            in_specs=[
                pl.BlockSpec((1, entries, STEP), lambda i, w: (i, 0, 0)),
                whole(atom_scale),
                whole(params),
                pl.BlockSpec((1, 1, 128), lambda i, w: (w[at + 2 * SIDE], 0, 0)),
                pl.BlockSpec((1, 1, 128), lambda i, w: (w[at + 2 * SIDE + 1], 0, 0)),
                *[whole(x) for x in pieces],
            ],
            out_specs=pl.BlockSpec((8, CHUNK), lambda i, w: (0, 0)),
            scratch_shapes=[
                pltpu.VMEM((2 * CHUNK, entries), BF),
                pltpu.VMEM((CHUNK, 128), F32),
                pltpu.VMEM((2 * CHUNK, TILE), F32),
                pltpu.VMEM((2 * CHUNK, TILE), F32),
                pltpu.VMEM((CHUNK, 128), F32),
                pltpu.VMEM((CHUNK, 128), F32),
            ],
        ),
        out_shape=jax.ShapeDtypeStruct((8, CHUNK), F32),
        compiler_params=pltpu.CompilerParams(dimension_semantics=("arbitrary",)),
        cost_estimate=pl.CostEstimate(
            flops=4 * atoms * entries * CHUNK,
            transcendentals=2 * atoms * CHUNK,
            bytes_accessed=atoms * entries * 2 + entries * CHUNK * 2,
        ),
        name="match",
    )(where, dictionary, atom_scale, params, kappa_a, kappa_b, *pieces)


ORDER = (0, -1, 1, 2)


def output_order():
    i = jnp.arange(8 * NRO, dtype=jnp.int32)[:, None]
    half, one, two, column, y = i // 512, i // 128 % 4, i // 32 % 4, i // 8 % 4, i % 8
    x = jnp.where(half == 0, two, one)
    z = jnp.where(half == 0, one, two)
    target = y * NRO + (x * SIDE + z) * 8 + half * 4 + column
    return (target == jnp.arange(8 * NRO, dtype=jnp.int32)[None, :]).astype(BF)


def finish_kernel(s_ref, e_ref, o_ref):
    found = []
    for kind in range(2):
        for place in range(SIDE):
            parts = []
            for source in range(SIDE * SIDE):
                own = source % SIDE if kind == 0 else source // SIDE
                k = ORDER.index((place - own + 1) % SIDE - 1)
                parts.append(s_ref[source, k, :, 128 * kind : 128 * kind + 128])
            top = parts[0][7:8]
            for p in parts[1:]:
                top = jnp.maximum(top, p[7:8])
            total = jnp.zeros_like(parts[0])
            for p in parts:
                total = total + p * jnp.exp(p[7:8] - top)
            row = lax.broadcasted_iota(jnp.int32, total.shape, 0)
            found.append(jnp.where(row < 6, total / total[6:7], 0.0))
    found = jnp.concatenate(found, axis=1)
    high = found.astype(BF).astype(F32)
    middle = (found - high).astype(BF).astype(F32)
    low = found - high - middle
    parts = jnp.concatenate([high, middle, low, jnp.zeros_like(low)], axis=0).astype(BF)
    moved = jnp.dot(parts, e_ref[...], preferred_element_type=F32)
    o_ref[...] = (moved[:8] + moved[8:16] + moved[16:24])[:6]


def finish(stats, order):
    return pl.pallas_call(
        finish_kernel,
        out_shape=jax.ShapeDtypeStruct((6, 8 * NRO), F32),
        name="finish",
    )(stats, order)


def shift(v, axis, by):
    return lax.ppermute(v, axis, [(i, (i + by) % SIDE) for i in range(SIDE)])


def body(kspace, sampled_lines, sensitivity, dictionary, atom_params, concentration):
    peers = lax.axis_size("frame")
    mx, mz = lax.axis_index("cx"), lax.axis_index("cz")
    outgoing = transform_readout(kspace, sensitivity)
    received = lax.all_to_all(outgoing, COIL, split_axis=0, concat_axis=0, tiled=True)

    split, atom_scale = split_dictionary(dictionary)
    atoms = dictionary.shape[0]
    high = lax.reduce_precision(atom_params, 8, 7)
    ones = jnp.ones((1, atoms), F32)
    none = jnp.zeros((1, atoms), F32)
    params = jnp.concatenate([high, ones, none, atom_params - high, none, none], axis=0)
    params = jnp.pad(params.T.astype(BF), ((0, 0), (0, 112)))
    params = params.reshape(atoms // STEP, 2, TILE, 128)
    weights = phase_weights(sampled_lines)
    kappa = concentration.reshape(8, SIDE, SIDE, 2, 4)
    kappa_a = kappa[:, :, :, 0].transpose(2, 1, 3, 0).reshape(SIDE, 1, 128)
    kappa_b = kappa[:, :, :, 1].transpose(1, 2, 3, 0).reshape(SIDE, 1, 128)
    own = jnp.arange(4 * 10, dtype=jnp.int32)
    kind, step = own % 10, own // 10
    along_x = (kind < 4) | (kind == 9)
    index = jnp.where(kind < 8, kind % 4, step)
    moved = jnp.where(index == 1, -1, jnp.where(index == 2, 1, jnp.where(index == 3, 2, 0)))
    where = (jnp.where(along_x, mx, mz) + moved + SIDE) % SIDE
    received, split, atom_scale, params, weights, kappa_a, kappa_b, where, final_order = (
        lax.optimization_barrier(
            (
                received,
                split,
                atom_scale,
                params,
                weights,
                kappa_a,
                kappa_b,
                where,
                output_order(),
            )
        )
    )

    sent = reconstruct(received, weights, peers)
    shares = lax.all_to_all(sent, "frame", split_axis=0, concat_axis=0, tiled=True)

    def first(v, axis):
        return jnp.stack([v, shift(v, axis, 1), shift(v, axis, -1), shift(v, axis, 2)])

    a = first(shares[:, 0], "cx")
    b = first(shares[:, 1], "cz")
    a_less, b_less = shift(a, "cz", 1), shift(b, "cx", 1)
    a_more, b_more = shift(a, "cz", -1), shift(b, "cx", -1)
    a_far = [shift(a_less[:2], "cz", 1), shift(a_more[2:], "cz", -1)]
    b_far = [shift(b_less[:2], "cx", 1), shift(b_more[2:], "cx", -1)]

    def chunk(k, pieces, place):
        return match(split, atom_scale, params, kappa_a, kappa_b, where, pieces, place, k)

    two = ((0, 0), (1, 0))
    stats = [
        chunk(0, [a, b], two),
        chunk(1, [a_less, b_less], two),
        chunk(2, [a_more, b_more], two),
        chunk(3, [*a_far, *b_far], ((0, 0), (0, 2), (1, 0), (1, 2))),
    ]
    stats = jnp.stack(stats)
    sources = SIDE * SIDE
    stats = lax.all_to_all(
        jnp.broadcast_to(stats[None], (sources, *stats.shape)), COIL, 0, 0, tiled=True
    )
    return finish(stats, final_order)


def solution(mesh):
    split = Mesh(mesh.devices.reshape(SIDE, SIDE, mesh.shape["frame"]), (*COIL, "frame"))
    return jax.shard_map(
        body,
        mesh=split,
        in_specs=(
            P(COIL, "frame", None, None),
            P("frame", None),
            P(COIL, None, None),
            P(COIL, None),
            P(None, COIL),
            P("frame"),
        ),
        out_specs=P(None, "frame"),
        check_vma=False,
    )
```

```python
import functools
import math

import jax
import jax.numpy as jnp
from jax import lax
from jax.experimental import pallas as pl
from jax.experimental.pallas import tpu as pltpu
from jax.sharding import Mesh
from jax.sharding import PartitionSpec as P

NPE = 64
NRO = 128
ROWS = 64
LINES = 8
SIDE = 4
GROUP = 4
CHUNK = 256
STEP = 512
COIL = ("cx", "cz")
BF = jnp.bfloat16
F32 = jnp.float32
NT = (((1,), (1,)), ((), ()))


def readout_table():
    position = jnp.arange(NRO, dtype=jnp.int32)
    angles = (position[:, None] * position[None, :] % NRO).astype(F32) * (2.0 * math.pi / NRO)
    return jnp.concatenate([jnp.cos(angles), -jnp.sin(angles)], axis=1).astype(BF)


def phase_weights(line_index):
    rows = jnp.arange(ROWS, dtype=jnp.int32)
    angles = (line_index[:, :, None] * rows[None, None, :] % NPE).astype(F32) * (2.0 * math.pi / NPE)
    groups = line_index.shape[0] // GROUP
    c = jnp.cos(angles).reshape(groups, GROUP * LINES, ROWS)
    s = jnp.sin(angles).reshape(groups, GROUP * LINES, ROWS)
    base = jnp.concatenate(
        [jnp.concatenate([c, s, s, -c], axis=2), jnp.concatenate([-s, c, c, s], axis=2)], axis=1
    )
    high = lax.reduce_precision(base, 8, 7)
    return jnp.concatenate([high, base - high], axis=1).astype(BF)


def split_kernel(d_ref, q_ref, o_ref, a_ref):
    entries = d_ref.shape[1]
    half = entries // 2
    total = jnp.zeros((8, d_ref.shape[0]), F32)
    for b in range(entries // 256):
        block = d_ref[:, 256 * b : 256 * b + 256]
        turned = lax.dot_general(q_ref[...], block, NT, preferred_element_type=F32)
        o_ref[0, 128 * b : 128 * b + 128] = turned[:128].astype(BF)
        o_ref[0, half + 128 * b : half + 128 * b + 128] = turned[128:].astype(BF)
        total = total + jnp.sum((turned * turned).reshape(32, 8, -1), axis=0)
    mean = jnp.sum(total, axis=0, keepdims=True) * (1.0 / entries)
    a_ref[0] = jnp.broadcast_to(lax.rsqrt(mean + 1e-06), a_ref.shape[1:])


def split_dictionary(dictionary):
    atoms, entries = dictionary.shape
    row = jnp.arange(256, dtype=jnp.int32)[:, None]
    col = jnp.arange(256, dtype=jnp.int32)[None, :]
    q = (col == 2 * (row % 128) + row // 128).astype(BF)
    steps = atoms // STEP
    return pl.pallas_call(
        split_kernel,
        grid=(steps,),
        in_specs=[
            pl.BlockSpec((STEP, entries), lambda i: (i, 0)),
            pl.BlockSpec((256, 256), lambda i: (0, 0)),
        ],
        out_specs=[
            pl.BlockSpec((1, entries, STEP), lambda i: (i, 0, 0)),
            pl.BlockSpec((1, 8, STEP), lambda i: (i, 0, 0)),
        ],
        out_shape=[
            jax.ShapeDtypeStruct((steps, entries, STEP), BF),
            jax.ShapeDtypeStruct((steps, 8, STEP), F32),
        ],
        cost_estimate=pl.CostEstimate(
            flops=2 * atoms * entries * 256, transcendentals=0, bytes_accessed=atoms * entries * 4
        ),
        name="split_dictionary",
    )(dictionary, q)


def readout_kernel(k_ref, t_ref, s_ref, o_ref):
    coils, rows, _ = k_ref.shape
    dests = o_ref.shape[0]
    per = GROUP * LINES
    step = 4
    low_lane = lax.broadcasted_iota(jnp.int32, (NRO, step * 128), 1) % 128 < 64

    def some_groups(i, carry):
        pieces = []
        for c in range(coils):
            k = k_ref[c, pl.ds(pl.multiple_of(i * step * per, step * per), step * per), :]
            turned = jnp.concatenate([k[:, NRO:], -k[:, :NRO]], axis=1)
            k = k.reshape(step, per, 2 * NRO)
            turned = turned.reshape(step, per, 2 * NRO)
            stacked = jnp.stack([k, turned, k, turned], axis=1).reshape(step * 128, 2 * NRO)
            out = lax.dot_general(t_ref[...], stacked, NT, preferred_element_type=F32)
            high = out.astype(BF).astype(F32)
            pieces.append(jnp.where(low_lane, high, out - high))
        lanes = pl.ds(pl.multiple_of(i * step * 128, step * 128), step * 128)
        for d in range(dests):
            both = jnp.concatenate([p[8 * d : 8 * d + 8] for p in pieces], axis=0)
            o_ref[d, :, lanes] = both.astype(BF)
        return carry

    lax.fori_loop(0, rows // (step * per), some_groups, 0)
    base = rows // per * 128
    for r in range(2):
        pieces = []
        for c in range(coils):
            s = jnp.concatenate(
                [s_ref[c, r : r + 1, NRO * y : NRO * y + NRO] for y in range(ROWS)], axis=0
            )
            high = s.astype(BF).astype(F32)
            pieces.append(jnp.concatenate([high, s - high], axis=0).T)
        for d in range(dests):
            both = jnp.concatenate([p[8 * d : 8 * d + 8] for p in pieces], axis=0)
            o_ref[d, :, base + 128 * r : base + 128 * r + 128] = both.astype(BF)


def transform_readout(kspace, sensitivity):
    coils, frames = kspace.shape[:2]
    width = frames // GROUP * 128 + 256
    return pl.pallas_call(
        readout_kernel,
        out_shape=jax.ShapeDtypeStruct((SIDE * SIDE, coils * 8, width), BF),
        name="transform_readout",
    )(
        kspace.reshape(coils, frames * LINES, 2 * NRO),
        readout_table(),
        sensitivity,
    )


def recon_kernel(r_ref, w_ref, o_ref, s1_ref, s2_ref, comb_ref):
    sources, sub, width = r_ref.shape
    rows = sources * sub
    coils = rows // 8
    groups = (width - 256) // 128
    for r, ref in ((0, s1_ref), (1, s2_ref)):
        at = width - 256 + 128 * r
        parts = r_ref[:, :, at : at + 128].reshape(rows, 128).astype(F32)
        ref[...] = parts + pltpu.roll(parts, 64, 1)
    frame_of_row = lax.broadcasted_iota(jnp.int32, (64, 256), 0) // LINES % GROUP
    zero = jnp.zeros((64, 256), BF)

    def one_group(g):
        lhs = r_ref[:, :, pl.ds(pl.multiple_of(g * 128, 128), 128)].reshape(rows, 128)
        lhs = jnp.concatenate([lhs, lhs], axis=1)
        high = w_ref[g, :64]
        low = w_ref[g, 64:]
        for j in range(GROUP):
            mine = frame_of_row == j
            h = jnp.where(mine, high, zero)
            w = jnp.concatenate([h, h, jnp.where(mine, low, zero), zero], axis=0)
            image = jnp.dot(lhs, w, preferred_element_type=F32)
            total = s1_ref[...] * image[:, :128] + s2_ref[...] * image[:, 128:]
            comb_ref[pl.ds(pl.multiple_of((g * GROUP + j) * 8, 8), 8), :] = jnp.sum(
                total.reshape(coils, 8, 128), axis=0
            )

    def some_groups(i, carry):
        for k in range(4):
            one_group(4 * i + k)
        return carry

    lax.fori_loop(0, groups // 4, some_groups, 0)
    frames = groups * GROUP
    for pair in range(4):
        t = [comb_ref[pl.ds(2 * pair + k, frames, stride=8), :].T for k in range(2)]
        half, at = pair // 2, pair % 2 * 16
        for dest in range(o_ref.shape[0]):
            for r in range(2):
                y = r * ROWS + 8 * dest
                both = jnp.concatenate([t[0][y : y + 8], t[1][y : y + 8]], axis=0)
                o_ref[dest, half, r, at : at + 16, :] = both.astype(BF)


def reconstruct(received, weights, peers):
    sources, sub, width = received.shape
    frames = (width - 256) // 128 * GROUP
    rows = sources * sub
    return pl.pallas_call(
        recon_kernel,
        out_shape=jax.ShapeDtypeStruct((peers, 2, 2, 32, frames), BF),
        scratch_shapes=[
            pltpu.VMEM((rows, 128), F32),
            pltpu.VMEM((rows, 128), F32),
            pltpu.VMEM((frames * 8, 128), F32),
        ],
        name="reconstruct",
    )(received, weights)


def match_kernel(count, chunks, at_ref, d_ref, a_ref, p_ref, ca_ref, cb_ref, *refs):
    pieces = refs[:count]
    o_ref, n_ref, u_ref, q_ref, m_ref, acc_ref = refs[count:]
    step = pl.program_id(0)
    voxels, half = n_ref.shape
    wide = STEP // 128

    def part(f, r):
        rows = [ref[i, f, r] for ref in pieces for i in range(ref.shape[0])]
        return jnp.concatenate(rows, axis=0)

    def fingerprints(r):
        return jnp.concatenate([part(f, r) for f in range(pieces[0].shape[1])], axis=1)

    def inner():
        re = fingerprints(0)
        im = fingerprints(1)
        rows = jnp.concatenate(
            [
                jnp.concatenate([re, im], axis=1),
                jnp.concatenate([im, n_ref[...]], axis=1),
            ],
            axis=0,
        )
        out = jnp.dot(rows, d_ref[0], preferred_element_type=F32)
        q_ref[...] = out[:voxels] * out[:voxels] + out[voxels:] * out[voxels:]

    def weigh(before):
        u = u_ref[...]
        scale = a_ref[before, :1]
        params = p_ref[before]
        logits = jnp.sqrt(q_ref[...]) * scale * jnp.concatenate([u] * wide, axis=1)
        old = m_ref[...]
        top = logits[:, :128]
        for k in range(1, wide):
            top = jnp.maximum(top, logits[:, 128 * k : 128 * k + 128])
        top = jnp.maximum(old, jnp.max(top, axis=1, keepdims=True))
        m_ref[...] = top
        weights = jnp.exp(logits - jnp.concatenate([top] * wide, axis=1))
        high = weights.astype(BF)
        low = (weights - high.astype(F32)).astype(BF)
        acc_ref[...] = (
            acc_ref[...] * jnp.exp(old - top)
            + jnp.dot(high, params, preferred_element_type=F32)
            + jnp.dot(low, params, preferred_element_type=F32)
        )

    @pl.when(step == 0)
    def _():
        total = jnp.zeros((voxels, 128), F32)
        for f in range(pieces[0].shape[1]):
            re = part(f, 0)
            im = part(f, 1).astype(F32)
            n_ref[:, 128 * f : 128 * f + 128] = -re
            re = re.astype(F32)
            total = total + re * re + im * im
        mean = jnp.sum(total, axis=1, keepdims=True) * (1.0 / (2 * half))
        scale = lax.rsqrt(mean + 1e-06) * (1.0 / (2 * half))
        kappas = []
        for c in chunks:
            for kind, ref in ((0, ca_ref), (1, cb_ref)):
                row = jnp.broadcast_to(ref[at_ref[2 + 2 * c + kind]], (8, 128))
                kappas.append(pltpu.roll(row, 128 - 32 * at_ref[kind], 1)[:1])
        kappa = jnp.broadcast_to(jnp.concatenate(kappas, axis=1), (128, voxels)).T
        u_ref[...] = scale * kappa
        m_ref[...] = jnp.zeros_like(m_ref)
        acc_ref[...] = jnp.zeros_like(acc_ref)
        inner()

    @pl.when(step > 0)
    def _():
        weigh(step - 1)
        inner()

    @pl.when(step == pl.num_programs(0) - 1)
    def _():
        weigh(step)
        acc = acc_ref[...].T
        sums = acc[:8] + acc[8:16]
        row = lax.broadcasted_iota(jnp.int32, sums.shape, 0)
        sums = jnp.where(row == 7, m_ref[...].T[:8], sums)
        for k in range(2 * len(chunks)):
            block = sums[:, 128 * k : 128 * k + 128]
            o_ref[:, 128 * k : 128 * k + 128] = pltpu.roll(block, 32 * at_ref[k % 2], 1)


def match(dictionary, atom_scale, params, kappa_a, kappa_b, where, chunks, pieces):
    steps, entries, _ = dictionary.shape
    atoms = steps * STEP
    voxels = CHUNK * len(chunks)
    whole = lambda x: pl.BlockSpec(x.shape, lambda i, w, n=x.ndim: (0,) * n)
    return pl.pallas_call(
        functools.partial(match_kernel, len(pieces), chunks),
        grid_spec=pltpu.PrefetchScalarGridSpec(
            num_scalar_prefetch=1,
            grid=(steps,),
            in_specs=[
                pl.BlockSpec((1, entries, STEP), lambda i, w: (i, 0, 0)),
                *[whole(x) for x in (atom_scale, params, kappa_a, kappa_b, *pieces)],
            ],
            out_specs=pl.BlockSpec((8, voxels), lambda i, w: (0, 0)),
            scratch_shapes=[
                pltpu.VMEM((voxels, entries // 2), BF),
                pltpu.VMEM((voxels, 128), F32),
                pltpu.VMEM((voxels, STEP), F32),
                pltpu.VMEM((voxels, 128), F32),
                pltpu.VMEM((voxels, 128), F32),
            ],
        ),
        out_shape=jax.ShapeDtypeStruct((8, voxels), F32),
        compiler_params=pltpu.CompilerParams(dimension_semantics=("arbitrary",)),
        cost_estimate=pl.CostEstimate(
            flops=4 * atoms * entries * voxels,
            transcendentals=2 * atoms * voxels,
            bytes_accessed=atoms * entries * 2 + entries * voxels * 2,
        ),
        name="match",
    )(where, dictionary, atom_scale, params, kappa_a, kappa_b, *pieces)


ORDER = (0, 3, 1, 2)


def output_order():
    i = jnp.arange(8 * NRO, dtype=jnp.int32)[:, None]
    half, one, two, column, y = i // 512, i // 128 % 4, i // 32 % 4, i // 8 % 4, i % 8
    x = jnp.where(half == 0, two, one)
    z = jnp.where(half == 0, one, two)
    target = y * NRO + (x * SIDE + z) * 8 + half * 4 + column
    return (target == jnp.arange(8 * NRO, dtype=jnp.int32)[None, :]).astype(BF)


def finish_kernel(s_ref, e_ref, o_ref):
    found = []
    for kind in range(2):
        for place in range(SIDE):
            parts = []
            for source in range(SIDE * SIDE):
                own = source % SIDE if kind == 0 else source // SIDE
                k = ORDER.index((place - own) % SIDE)
                at = (2 * k + kind) * 128
                parts.append(s_ref[source, :, at : at + 128])
            top = parts[0][7:8]
            for p in parts[1:]:
                top = jnp.maximum(top, p[7:8])
            total = jnp.zeros_like(parts[0])
            for p in parts:
                total = total + p * jnp.exp(p[7:8] - top)
            row = lax.broadcasted_iota(jnp.int32, total.shape, 0)
            found.append(jnp.where(row < 6, total / total[6:7], 0.0))
    found = jnp.concatenate(found, axis=1)
    high = found.astype(BF).astype(F32)
    middle = (found - high).astype(BF).astype(F32)
    low = found - high - middle
    parts = jnp.concatenate([high, middle, low, jnp.zeros_like(low)], axis=0).astype(BF)
    moved = jnp.dot(parts, e_ref[...], preferred_element_type=F32)
    o_ref[...] = (moved[:8] + moved[8:16] + moved[16:24])[:6]


def finish(stats, order):
    return pl.pallas_call(
        finish_kernel,
        out_shape=jax.ShapeDtypeStruct((6, 8 * NRO), F32),
        name="finish",
    )(stats, order)


def shift(v, axis, by):
    return lax.ppermute(v, axis, [(i, (i + by) % SIDE) for i in range(SIDE)])


def body(kspace, sampled_lines, sensitivity, dictionary, atom_params, concentration):
    peers = lax.axis_size("frame")
    mx, mz = lax.axis_index("cx"), lax.axis_index("cz")
    outgoing = transform_readout(kspace, sensitivity)
    received = lax.all_to_all(outgoing, COIL, split_axis=0, concat_axis=0, tiled=True)

    split, atom_scale = split_dictionary(dictionary)
    atoms = dictionary.shape[0]
    high = lax.reduce_precision(atom_params, 8, 7)
    ones = jnp.ones((1, atoms), F32)
    none = jnp.zeros((1, atoms), F32)
    params = jnp.concatenate([high, ones, none, atom_params - high, none, none], axis=0)
    params = jnp.pad(params.T.astype(BF), ((0, 0), (0, 112)))
    params = params.reshape(atoms // STEP, STEP, 128)
    weights = phase_weights(sampled_lines)
    kappa = concentration.reshape(8, SIDE, SIDE, 2, 4)
    kappa_a = kappa[:, :, :, 0].transpose(2, 1, 3, 0).reshape(SIDE, 1, 128)
    kappa_b = kappa[:, :, :, 1].transpose(1, 2, 3, 0).reshape(SIDE, 1, 128)
    entry = jnp.arange(2 + 2 * SIDE, dtype=jnp.int32)
    index = entry // 2 - 1
    on = jnp.where(index == 1, ORDER[1], jnp.where(index == 2, ORDER[2], 0))
    on = jnp.where(index == 3, ORDER[3], on)
    along_x = (entry == 0) | ((entry > 1) & (entry % 2 == 1))
    where = (jnp.where(along_x, mx, mz) + on) % SIDE
    received, split, atom_scale, params, weights, kappa_a, kappa_b, where, final_order = (
        lax.optimization_barrier(
            (
                received,
                split,
                atom_scale,
                params,
                weights,
                kappa_a,
                kappa_b,
                where,
                output_order(),
            )
        )
    )

    sent = reconstruct(received, weights, peers)
    shares = lax.all_to_all(sent, "frame", split_axis=0, concat_axis=0, tiled=True)

    def first(v, axis):
        return jnp.stack([v, shift(v, axis, -1), shift(v, axis, 2), shift(v, axis, 1)])

    a = first(shares[:, 0], "cx")
    b = first(shares[:, 1], "cz")
    a_less, b_less = shift(a, "cz", 1), shift(b, "cx", 1)
    a_more, b_more = shift(a, "cz", -1), shift(b, "cx", -1)
    a_far = [shift(a_less[:2], "cz", 1), shift(a_more[2:], "cz", -1)]
    b_far = [shift(b_less[:2], "cx", 1), shift(b_more[2:], "cx", -1)]

    common = (split, atom_scale, params, kappa_a, kappa_b, where)
    stats = jnp.concatenate(
        [
            match(*common, (0,), [a, b]),
            match(*common, (1, 2), [a_less, b_less, a_more, b_more]),
            match(*common, (3,), [*a_far, *b_far]),
        ],
        axis=1,
    )
    sources = SIDE * SIDE
    stats = lax.all_to_all(
        jnp.broadcast_to(stats[None], (sources, *stats.shape)), COIL, 0, 0, tiled=True
    )
    return finish(stats, final_order)


def solution(mesh):
    split = Mesh(mesh.devices.reshape(SIDE, SIDE, mesh.shape["frame"]), (*COIL, "frame"))
    return jax.shard_map(
        body,
        mesh=split,
        in_specs=(
            P(COIL, "frame", None, None),
            P("frame", None),
            P(COIL, None, None),
            P(COIL, None),
            P(None, COIL),
            P("frame"),
        ),
        out_specs=P(None, "frame"),
        check_vma=False,
    )
```

```python
import functools
import math

import jax
import jax.numpy as jnp
from jax import lax
from jax.experimental import pallas as pl
from jax.experimental.pallas import tpu as pltpu
from jax.sharding import Mesh
from jax.sharding import PartitionSpec as P

NPE = 64
NRO = 128
ROWS = 64
LINES = 8
SIDE = 4
GROUP = 4
CHUNK = 256
STEP = 512
COIL = ("cx", "cz")
BF = jnp.bfloat16
F32 = jnp.float32
NT = (((1,), (1,)), ((), ()))
HELD = pl.BlockSpec(memory_space=pltpu.VMEM)
ROOM = 16 << 20


def readout_table():
    position = jnp.arange(NRO, dtype=jnp.int32)
    angles = (position[:, None] * position[None, :] % NRO).astype(F32) * (2.0 * math.pi / NRO)
    return jnp.concatenate([jnp.cos(angles), -jnp.sin(angles)], axis=1).astype(BF)


def phase_weights(line_index):
    rows = jnp.arange(ROWS, dtype=jnp.int32)
    angles = (line_index[:, :, None] * rows[None, None, :] % NPE).astype(F32) * (2.0 * math.pi / NPE)
    groups = line_index.shape[0] // GROUP
    c = jnp.cos(angles).reshape(groups, GROUP * LINES, ROWS)
    s = jnp.sin(angles).reshape(groups, GROUP * LINES, ROWS)
    base = jnp.concatenate(
        [jnp.concatenate([c, s, s, -c], axis=2), jnp.concatenate([-s, c, c, s], axis=2)], axis=1
    )
    high = lax.reduce_precision(base, 8, 7)
    return jnp.concatenate([high, base - high], axis=1).astype(BF)


def split_kernel(d_ref, q_ref, o_ref, a_ref):
    entries = d_ref.shape[1]
    half = entries // 2
    step = pl.program_id(0)
    total = jnp.zeros((8, d_ref.shape[0]), F32)
    for b in range(entries // 256):
        block = d_ref[:, 256 * b : 256 * b + 256]
        turned = lax.dot_general(q_ref[...], block, NT, preferred_element_type=F32)
        o_ref[0, 128 * b : 128 * b + 128] = turned[:128].astype(BF)
        o_ref[0, half + 128 * b : half + 128 * b + 128] = turned[128:].astype(BF)
        total = total + jnp.sum((turned * turned).reshape(32, 8, -1), axis=0)
    mean = jnp.sum(total, axis=0, keepdims=True) * (1.0 / entries)
    a_ref[step] = jnp.broadcast_to(lax.rsqrt(mean + 1e-06), a_ref.shape[1:])


def split_dictionary(dictionary):
    atoms, entries = dictionary.shape
    row = jnp.arange(256, dtype=jnp.int32)[:, None]
    col = jnp.arange(256, dtype=jnp.int32)[None, :]
    q = (col == 2 * (row % 128) + row // 128).astype(BF)
    steps = atoms // STEP
    return pl.pallas_call(
        split_kernel,
        grid=(steps,),
        in_specs=[
            pl.BlockSpec((STEP, entries), lambda i: (i, 0)),
            pl.BlockSpec((256, 256), lambda i: (0, 0)),
        ],
        out_specs=[pl.BlockSpec((1, entries, STEP), lambda i: (i, 0, 0)), HELD],
        out_shape=[
            jax.ShapeDtypeStruct((steps, entries, STEP), BF),
            jax.ShapeDtypeStruct((steps, 8, STEP), F32),
        ],
        cost_estimate=pl.CostEstimate(
            flops=2 * atoms * entries * 256, transcendentals=0, bytes_accessed=atoms * entries * 4
        ),
        name="split_dictionary",
    )(dictionary, q)


def readout_kernel(k_ref, t_ref, s_ref, o_ref):
    coils, rows, _ = k_ref.shape
    dests = o_ref.shape[0]
    per = GROUP * LINES
    step = 4
    low_lane = lax.broadcasted_iota(jnp.int32, (NRO, step * 128), 1) % 128 < 64

    def some_groups(i, carry):
        pieces = []
        for c in range(coils):
            k = k_ref[c, pl.ds(pl.multiple_of(i * step * per, step * per), step * per), :]
            turned = jnp.concatenate([k[:, NRO:], -k[:, :NRO]], axis=1)
            k = k.reshape(step, per, 2 * NRO)
            turned = turned.reshape(step, per, 2 * NRO)
            stacked = jnp.stack([k, turned, k, turned], axis=1).reshape(step * 128, 2 * NRO)
            out = lax.dot_general(t_ref[...], stacked, NT, preferred_element_type=F32)
            high = out.astype(BF).astype(F32)
            pieces.append(jnp.where(low_lane, high, out - high))
        lanes = pl.ds(pl.multiple_of(i * step * 128, step * 128), step * 128)
        for d in range(dests):
            both = jnp.concatenate([p[8 * d : 8 * d + 8] for p in pieces], axis=0)
            o_ref[d, :, lanes] = both.astype(BF)
        return carry

    lax.fori_loop(0, rows // (step * per), some_groups, 0)
    base = rows // per * 128
    for r in range(2):
        pieces = []
        for c in range(coils):
            s = jnp.concatenate(
                [s_ref[c, r : r + 1, NRO * y : NRO * y + NRO] for y in range(ROWS)], axis=0
            )
            high = s.astype(BF).astype(F32)
            pieces.append(jnp.concatenate([high, s - high], axis=0).T)
        for d in range(dests):
            both = jnp.concatenate([p[8 * d : 8 * d + 8] for p in pieces], axis=0)
            o_ref[d, :, base + 128 * r : base + 128 * r + 128] = both.astype(BF)


def transform_readout(kspace, sensitivity):
    coils, frames = kspace.shape[:2]
    width = frames // GROUP * 128 + 256
    return pl.pallas_call(
        readout_kernel,
        out_shape=jax.ShapeDtypeStruct((SIDE * SIDE, coils * 8, width), BF),
        name="transform_readout",
    )(
        kspace.reshape(coils, frames * LINES, 2 * NRO),
        readout_table(),
        sensitivity,
    )


def recon_kernel(r_ref, w_ref, o_ref, s1_ref, s2_ref, comb_ref):
    sources, sub, width = r_ref.shape
    rows = sources * sub
    coils = rows // 8
    here = w_ref.shape[0]
    frames = comb_ref.shape[0] // 8
    step = pl.program_id(0)

    @pl.when(step == 0)
    def _():
        for r, ref in ((0, s1_ref), (1, s2_ref)):
            at = width - 256 + 128 * r
            parts = r_ref[:, :, at : at + 128].reshape(rows, 128).astype(F32)
            ref[...] = parts + pltpu.roll(parts, 64, 1)

    frame_of_row = lax.broadcasted_iota(jnp.int32, (64, 256), 0) // LINES % GROUP
    zero = jnp.zeros((64, 256), BF)
    for k in range(here):
        g = step * here + k
        lhs = r_ref[:, :, pl.ds(pl.multiple_of(g * 128, 128), 128)].reshape(rows, 128)
        lhs = jnp.concatenate([lhs, lhs], axis=1)
        high = w_ref[k, :64]
        low = w_ref[k, 64:]
        for j in range(GROUP):
            mine = frame_of_row == j
            h = jnp.where(mine, high, zero)
            w = jnp.concatenate([h, h, jnp.where(mine, low, zero), zero], axis=0)
            image = jnp.dot(lhs, w, preferred_element_type=F32)
            total = s1_ref[...] * image[:, :128] + s2_ref[...] * image[:, 128:]
            comb_ref[pl.ds(pl.multiple_of((g * GROUP + j) * 8, 8), 8), :] = jnp.sum(
                total.reshape(coils, 8, 128), axis=0
            )

    @pl.when(step == pl.num_programs(0) - 1)
    def _():
        for pair in range(4):
            t = [comb_ref[pl.ds(2 * pair + k, frames, stride=8), :].T for k in range(2)]
            half, at = pair // 2, pair % 2 * 16
            for dest in range(o_ref.shape[0]):
                for r in range(2):
                    y = r * ROWS + 8 * dest
                    both = jnp.concatenate([t[0][y : y + 8], t[1][y : y + 8]], axis=0)
                    o_ref[dest, half, r, at : at + 16, :] = both.astype(BF)


def reconstruct(received, weights, peers):
    sources, sub, width = received.shape
    groups = weights.shape[0]
    frames = groups * GROUP
    rows = sources * sub
    return pl.pallas_call(
        recon_kernel,
        grid=(groups // 4,),
        in_specs=[HELD, pl.BlockSpec((4, *weights.shape[1:]), lambda i: (i, 0, 0))],
        out_specs=HELD,
        out_shape=jax.ShapeDtypeStruct((peers, 2, 2, 32, frames), BF),
        scratch_shapes=[
            pltpu.VMEM((rows, 128), F32),
            pltpu.VMEM((rows, 128), F32),
            pltpu.VMEM((frames * 8, 128), F32),
        ],
        compiler_params=pltpu.CompilerParams(
            dimension_semantics=("arbitrary",), vmem_limit_bytes=ROOM
        ),
        name="reconstruct",
    )(received, weights)


def match_kernel(count, chunks, at_ref, d_ref, a_ref, p_ref, ca_ref, cb_ref, *refs):
    pieces = refs[:count]
    o_ref, n_ref, u_ref, q_ref, m_ref, acc_ref = refs[count:]
    step = pl.program_id(0)
    voxels, half = n_ref.shape
    wide = STEP // 128

    def part(f, r):
        rows = [ref[i, f, r] for ref in pieces for i in range(ref.shape[0])]
        return jnp.concatenate(rows, axis=0)

    def fingerprints(r):
        return jnp.concatenate([part(f, r) for f in range(pieces[0].shape[1])], axis=1)

    def inner():
        re = fingerprints(0)
        im = fingerprints(1)
        rows = jnp.concatenate(
            [
                jnp.concatenate([re, im], axis=1),
                jnp.concatenate([im, n_ref[...]], axis=1),
            ],
            axis=0,
        )
        out = jnp.dot(rows, d_ref[0], preferred_element_type=F32)
        q_ref[...] = out[:voxels] * out[:voxels] + out[voxels:] * out[voxels:]

    def weigh(before):
        u = u_ref[...]
        scale = a_ref[before, :1]
        params = p_ref[before]
        logits = jnp.sqrt(q_ref[...]) * scale * jnp.concatenate([u] * wide, axis=1)
        old = m_ref[...]
        top = logits[:, :128]
        for k in range(1, wide):
            top = jnp.maximum(top, logits[:, 128 * k : 128 * k + 128])
        top = jnp.maximum(old, jnp.max(top, axis=1, keepdims=True))
        m_ref[...] = top
        weights = jnp.exp(logits - jnp.concatenate([top] * wide, axis=1))
        high = weights.astype(BF)
        low = (weights - high.astype(F32)).astype(BF)
        acc_ref[...] = (
            acc_ref[...] * jnp.exp(old - top)
            + jnp.dot(high, params, preferred_element_type=F32)
            + jnp.dot(low, params, preferred_element_type=F32)
        )

    @pl.when(step == 0)
    def _():
        total = jnp.zeros((voxels, 128), F32)
        for f in range(pieces[0].shape[1]):
            re = part(f, 0)
            im = part(f, 1).astype(F32)
            n_ref[:, 128 * f : 128 * f + 128] = -re
            re = re.astype(F32)
            total = total + re * re + im * im
        mean = jnp.sum(total, axis=1, keepdims=True) * (1.0 / (2 * half))
        scale = lax.rsqrt(mean + 1e-06) * (1.0 / (2 * half))
        kappas = []
        for c in chunks:
            for kind, ref in ((0, ca_ref), (1, cb_ref)):
                row = jnp.broadcast_to(ref[at_ref[2 + 2 * c + kind]], (8, 128))
                kappas.append(pltpu.roll(row, 128 - 32 * at_ref[kind], 1)[:1])
        kappa = jnp.broadcast_to(jnp.concatenate(kappas, axis=1), (128, voxels)).T
        u_ref[...] = scale * kappa
        m_ref[...] = jnp.zeros_like(m_ref)
        acc_ref[...] = jnp.zeros_like(acc_ref)
        inner()

    @pl.when(step > 0)
    def _():
        weigh(step - 1)
        inner()

    @pl.when(step == pl.num_programs(0) - 1)
    def _():
        weigh(step)
        acc = acc_ref[...].T
        sums = acc[:8] + acc[8:16]
        row = lax.broadcasted_iota(jnp.int32, sums.shape, 0)
        sums = jnp.where(row == 7, m_ref[...].T[:8], sums)
        for k in range(2 * len(chunks)):
            block = sums[:, 128 * k : 128 * k + 128]
            o_ref[:, 128 * k : 128 * k + 128] = pltpu.roll(block, 32 * at_ref[k % 2], 1)


def match(dictionary, atom_scale, params, kappa_a, kappa_b, where, chunks, pieces):
    steps, entries, _ = dictionary.shape
    atoms = steps * STEP
    voxels = CHUNK * len(chunks)
    return pl.pallas_call(
        functools.partial(match_kernel, len(pieces), chunks),
        grid_spec=pltpu.PrefetchScalarGridSpec(
            num_scalar_prefetch=1,
            grid=(steps,),
            in_specs=[
                pl.BlockSpec((1, entries, STEP), lambda i, w: (i, 0, 0)),
                *[HELD] * (4 + len(pieces)),
            ],
            out_specs=HELD,
            scratch_shapes=[
                pltpu.VMEM((voxels, entries // 2), BF),
                pltpu.VMEM((voxels, 128), F32),
                pltpu.VMEM((voxels, STEP), F32),
                pltpu.VMEM((voxels, 128), F32),
                pltpu.VMEM((voxels, 128), F32),
            ],
        ),
        out_shape=jax.ShapeDtypeStruct((8, voxels), F32),
        compiler_params=pltpu.CompilerParams(
            dimension_semantics=("arbitrary",), vmem_limit_bytes=ROOM
        ),
        cost_estimate=pl.CostEstimate(
            flops=4 * atoms * entries * voxels,
            transcendentals=2 * atoms * voxels,
            bytes_accessed=atoms * entries * 2 + entries * voxels * 2,
        ),
        name="match",
    )(where, dictionary, atom_scale, params, kappa_a, kappa_b, *pieces)


ORDER = (0, 3, 1, 2)


def output_order():
    i = jnp.arange(8 * NRO, dtype=jnp.int32)[:, None]
    half, one, two, column, y = i // 512, i // 128 % 4, i // 32 % 4, i // 8 % 4, i % 8
    x = jnp.where(half == 0, two, one)
    z = jnp.where(half == 0, one, two)
    target = y * NRO + (x * SIDE + z) * 8 + half * 4 + column
    return (target == jnp.arange(8 * NRO, dtype=jnp.int32)[None, :]).astype(BF)


def finish_kernel(s_ref, e_ref, o_ref):
    found = []
    for kind in range(2):
        for place in range(SIDE):
            parts = []
            for source in range(SIDE * SIDE):
                own = source % SIDE if kind == 0 else source // SIDE
                k = ORDER.index((place - own) % SIDE)
                at = (2 * k + kind) * 128
                parts.append(s_ref[source, :, at : at + 128])
            top = parts[0][7:8]
            for p in parts[1:]:
                top = jnp.maximum(top, p[7:8])
            total = jnp.zeros_like(parts[0])
            for p in parts:
                total = total + p * jnp.exp(p[7:8] - top)
            row = lax.broadcasted_iota(jnp.int32, total.shape, 0)
            found.append(jnp.where(row < 6, total / total[6:7], 0.0))
    found = jnp.concatenate(found, axis=1)
    high = found.astype(BF).astype(F32)
    middle = (found - high).astype(BF).astype(F32)
    low = found - high - middle
    parts = jnp.concatenate([high, middle, low, jnp.zeros_like(low)], axis=0).astype(BF)
    moved = jnp.dot(parts, e_ref[...], preferred_element_type=F32)
    o_ref[...] = (moved[:8] + moved[8:16] + moved[16:24])[:6]


def finish(stats, order):
    return pl.pallas_call(
        finish_kernel,
        in_specs=[HELD, HELD],
        out_shape=jax.ShapeDtypeStruct((6, 8 * NRO), F32),
        compiler_params=pltpu.CompilerParams(vmem_limit_bytes=ROOM),
        name="finish",
    )(stats, order)


def shift(v, axis, by):
    return lax.ppermute(v, axis, [(i, (i + by) % SIDE) for i in range(SIDE)])


def body(kspace, sampled_lines, sensitivity, dictionary, atom_params, concentration):
    peers = lax.axis_size("frame")
    mx, mz = lax.axis_index("cx"), lax.axis_index("cz")
    outgoing = transform_readout(kspace, sensitivity)
    received = lax.all_to_all(outgoing, COIL, split_axis=0, concat_axis=0, tiled=True)

    split, atom_scale = split_dictionary(dictionary)
    split = pltpu.with_memory_space_constraint(split, pltpu.HBM)
    atoms = dictionary.shape[0]
    high = lax.reduce_precision(atom_params, 8, 7)
    ones = jnp.ones((1, atoms), F32)
    none = jnp.zeros((1, atoms), F32)
    params = jnp.concatenate([high, ones, none, atom_params - high, none, none], axis=0)
    params = jnp.pad(params.T.astype(BF), ((0, 0), (0, 112)))
    params = params.reshape(atoms // STEP, STEP, 128)
    weights = phase_weights(sampled_lines)
    kappa = concentration.reshape(8, SIDE, SIDE, 2, 4)
    kappa_a = kappa[:, :, :, 0].transpose(2, 1, 3, 0).reshape(SIDE, 1, 128)
    kappa_b = kappa[:, :, :, 1].transpose(1, 2, 3, 0).reshape(SIDE, 1, 128)
    entry = jnp.arange(2 + 2 * SIDE, dtype=jnp.int32)
    index = entry // 2 - 1
    on = jnp.where(index == 1, ORDER[1], jnp.where(index == 2, ORDER[2], 0))
    on = jnp.where(index == 3, ORDER[3], on)
    along_x = (entry == 0) | ((entry > 1) & (entry % 2 == 1))
    where = (jnp.where(along_x, mx, mz) + on) % SIDE
    weights = pltpu.with_memory_space_constraint(weights, pltpu.HBM)
    received, weights = lax.optimization_barrier((received, weights))
    sent = reconstruct(received, weights, peers)
    shares = lax.all_to_all(sent, "frame", split_axis=0, concat_axis=0, tiled=True)
    common = (split, atom_scale, params, kappa_a, kappa_b, where)
    shares, common, final_order = lax.optimization_barrier((shares, common, output_order()))

    def first(v, axis):
        return jnp.stack([v, shift(v, axis, -1), shift(v, axis, 2), shift(v, axis, 1)])

    a = first(shares[:, 0], "cx")
    b = first(shares[:, 1], "cz")
    a_less, b_less = shift(a, "cz", 1), shift(b, "cx", 1)
    a_more, b_more = shift(a, "cz", -1), shift(b, "cx", -1)
    a_far = [shift(a_less[:2], "cz", 1), shift(a_more[2:], "cz", -1)]
    b_far = [shift(b_less[:2], "cx", 1), shift(b_more[2:], "cx", -1)]

    stats = jnp.concatenate(
        [
            match(*common, (0,), [a, b]),
            match(*common, (1, 2), [a_less, b_less, a_more, b_more]),
            match(*common, (3,), [*a_far, *b_far]),
        ],
        axis=1,
    )
    sources = SIDE * SIDE
    stats = lax.all_to_all(
        jnp.broadcast_to(stats[None], (sources, *stats.shape)), COIL, 0, 0, tiled=True
    )
    return finish(stats, final_order)


def solution(mesh):
    split = Mesh(mesh.devices.reshape(SIDE, SIDE, mesh.shape["frame"]), (*COIL, "frame"))
    return jax.shard_map(
        body,
        mesh=split,
        in_specs=(
            P(COIL, "frame", None, None),
            P("frame", None),
            P(COIL, None, None),
            P(COIL, None),
            P(None, COIL),
            P("frame"),
        ),
        out_specs=P(None, "frame"),
        check_vma=False,
    )
```
